512 devices in a mesh: narrow: 4 (over y_hi, core), wide: 128 (over z, x, y_lo).
Axes of the slice: x: 4, y: 8 (y_hi: 2, y_lo: 4; y = y_hi * 4 + y_lo), z: 8, core: 2. Of those that a mesh axis runs over, the one named last changes fastest.
Arguments:
- scan_pair: float32 [2, 4, 2048, 2048], P(None, None, 'wide', 'narrow'), may hold values from -6 to 6
Outputs:
- correlation: float32 [2, 4, 2048, 2048], P(None, None, 'wide', 'narrow')
The draws below stay inside these ranges and needn't reach their ends.
All inputs are finite; a program needn't handle non-finite values.
Results may differ from the reference program's by a relative error of at most 0.00015.
Values sent between devices are 32-bit elements; how exact they have to be, the bound alone decides.
A program may use at most 64 MiB of HBM per device.

```python
import jax
import jax.numpy as jnp
from jax import lax

XW = 4
NY = 2048
NZ = 2048


def block_levels(stream_key, shape, split, low, largest):
    loudness = 1.0
    for dim, parts in split:
        steps = jax.random.uniform(jax.random.fold_in(jax.random.fold_in(stream_key, 6), dim), (parts,), jnp.float32, low / len(split), largest / len(split))
        loudness = loudness * jnp.repeat(jnp.exp(steps), shape[dim] // parts).reshape((-1,) + (1,) * (len(shape) - 1 - dim))
    return loudness


def gaussian(rng, shape, deviation, reach, pieces=(), dtype=jnp.bfloat16):
    level = block_levels(rng, shape, pieces, -0.22, 0.18) if pieces else 1.0
    values = jax.random.normal(rng, shape, jnp.float32) * deviation * level
    return jnp.minimum(jnp.maximum(values, -reach), reach).astype(dtype)


def setup_inputs(seed: int = 0) -> dict:
    key_of = jax.random.split(jax.random.key(seed), 2)
    return {
        "scan_pair": gaussian(key_of[0], (2, XW, NZ, NY), 1.0, 6.0, ((2, 128), (3, 4)), jnp.float32),
    }


magnitude_floor = 0.25

def column(planes):
    packed = lax.complex(planes[0], planes[1])
    mirror = lax.complex(planes[2], planes[3])
    spectrum = jnp.fft.fft(packed, axis=1, norm='ortho')
    mirror_spectrum = jnp.fft.fft(mirror, axis=1, norm='ortho')
    own_real = jnp.real(spectrum)
    own_imag = jnp.imag(spectrum)
    twin_real = jnp.real(mirror_spectrum)
    twin_imag = jnp.imag(mirror_spectrum)
    first_real = (own_real + twin_real) * 0.5
    first_imag = (own_imag + twin_imag) * 0.5
    second_real = (own_imag - twin_imag) * 0.5
    second_imag = -(own_real - twin_real) * 0.5
    cross_real = first_real * second_real + first_imag * second_imag
    cross_imag = first_imag * second_real - first_real * second_imag
    modulus = jnp.maximum(jnp.sqrt(cross_real * cross_real + cross_imag * cross_imag), magnitude_floor)
    normalized = lax.complex(cross_real / modulus, cross_imag / modulus)
    result = jnp.fft.ifft(normalized, axis=1, norm='ortho')
    return jnp.stack([jnp.real(result), jnp.imag(result)])

def reference(scan_pair):
    swapped = jnp.swapaxes(scan_pair, 2, 3)
    real_plane = swapped[0]
    imag_plane = swapped[1]
    mirror_real = jnp.roll(jnp.flip(real_plane, (0, 1)), 1, axis=1)
    mirror_imag = -jnp.roll(jnp.flip(imag_plane, (0, 1)), 1, axis=1)
    stacked = jnp.stack([real_plane, imag_plane, mirror_real, mirror_imag], axis=1)
    result = lax.map(column, stacked)
    return jnp.swapaxes(jnp.moveaxis(result, 1, 0), 2, 3)
```

```python
import functools
import math

import jax
import jax.numpy as jnp
import numpy as np
from jax import lax
from jax.experimental import pallas as pl
from jax.experimental.pallas import tpu as pltpu
from jax.sharding import PartitionSpec as P

magnitude_floor = 0.25
MESH = pl.DeviceIdType.MESH

LINE, PLANE, LANES, ROWS = 16, 32, 128, 512
LENGTH, POINTS = 2048, 16


def constants():
    ka = np.arange(128)
    j = np.arange(128)
    z1 = (j % 8) * 16 + j // 8
    big = np.exp(-2j * np.pi * ((ka[:, None] * z1[None, :]) % 128) / 128)
    forward_big = np.concatenate([big.real, big.imag], axis=0)
    back = np.conj(big).T
    inverse_big = np.concatenate([back.real, back.imag], axis=0)

    z0 = np.arange(POINTS)
    small = np.exp(-2j * np.pi * ((z0[:, None] * z0[None, :]) % POINTS) / POINTS) / math.sqrt(LENGTH)

    def lanes(matrix, columns):
        block = np.einsum("xw,zk->xzwk", columns, matrix).reshape(64, 64)
        return np.block([[block.real, block.imag], [-block.imag, block.real]])

    same, reverse = np.eye(4), np.eye(4)[::-1]
    turn = np.exp(-2j * np.pi * ka[:, None] * z0[None, :] / LENGTH)
    turn = np.tile(turn, (1, 4))
    turn_real = np.concatenate([turn.real, turn.real], axis=1)
    turn_imag = np.concatenate([-turn.imag, turn.imag], axis=1)
    squares = np.stack(
        [
            lanes(small, same),
            lanes(small, reverse),
            lanes(np.conj(small), same),
            turn_real,
            turn_imag,
            np.eye(128)[::-1],
        ]
    )
    return (
        np.stack([forward_big, inverse_big]).astype(np.float32),
        squares.astype(np.float32),
    )


def dot(left, right):
    return jnp.dot(
        left, right, precision=lax.Precision.HIGHEST, preferred_element_type=jnp.float32
    )


def correlate(blocks, first_device, big_ref, square_ref, roll):
    def swap(value):
        return roll(value, 64, 1)

    lane = lax.broadcasted_iota(jnp.int32, (128, LANES), 1)
    real_lane = lane < 64
    sign = jnp.where(real_lane, -1.0, 1.0).astype(jnp.float32)
    turn_real, turn_imag = square_ref[3], square_ref[4]

    both = dot(big_ref[0], jnp.concatenate(blocks, axis=1))
    own, twin = [], []
    for n in range(4):
        upper = both[:128, n * 128 : (n + 1) * 128]
        lower = swap(both[128:, n * 128 : (n + 1) * 128])
        straight = upper + sign * lower
        conjugate = lower - sign * upper
        own.append(straight * turn_real + swap(straight) * turn_imag)
        twin.append(conjugate * turn_real + swap(conjugate) * turn_imag)
    mirrored = [
        jnp.where(first_device, twin[a], twin[b]) for a, b in ((0, 3), (3, 2), (2, 1), (1, 0))
    ]
    spectrum = dot(jnp.concatenate(own, axis=0), square_ref[0])
    mirror_spectrum = dot(jnp.concatenate(mirrored, axis=0), square_ref[1])
    normalized = []
    for n in range(4):
        s = spectrum[n * 128 : (n + 1) * 128]
        m = mirror_spectrum[n * 128 : (n + 1) * 128]
        first = (s + m) * 0.5
        half = (s - m) * 0.5
        turned = first * swap(half)
        plain = first * half
        cross = jnp.where(real_lane, turned - swap(turned), plain + swap(plain))
        square = cross * cross
        modulus = jnp.maximum(jnp.sqrt(square + swap(square)), magnitude_floor)
        normalized.append(cross / modulus)
    back = dot(jnp.concatenate(normalized, axis=0), square_ref[2])
    turned_back = []
    for n in range(4):
        value = back[n * 128 : (n + 1) * 128]
        turned_back.append(value * turn_real - swap(value) * turn_imag)
    both = dot(big_ref[1], jnp.concatenate(turned_back, axis=1))
    return [
        both[:128, n * 128 : (n + 1) * 128] + sign * swap(both[128:, n * 128 : (n + 1) * 128])
        for n in range(4)
    ]


def kernel(
    scan_ref, big_ref, square_ref, out_ref,
    rows, mid, landed, result, mid_back, landed_back,
    send_line, recv_line, send_plane, recv_plane,
    send_plane_back, recv_plane_back, send_line_back, recv_line_back, local,
):
    narrow, wide = lax.axis_index("narrow"), lax.axis_index("wide")
    y_hi, core = narrow // 2, narrow % 2
    z, sheet = wide // 16, wide % 16
    line = core * 8 + z
    plane = y_hi * 16 + sheet
    upper = narrow >= 2
    swap_matrix = square_ref[5]

    def line_peer(step):
        peer = (line + step) % LINE
        return peer, (y_hi * 2 + peer // 8, (peer % 8) * 16 + sheet)

    def plane_peer(step):
        peer = (plane + step) % PLANE
        return peer, ((peer // 16) * 2 + core, z * 16 + peer % 16)

    def exchange(count, peer_of, source, target, mine, send, recv, slot):
        def copy(step):
            peer, device = peer_of(step)
            return pltpu.make_async_remote_copy(
                src_ref=source(peer),
                dst_ref=target(mine),
                send_sem=send.at[step],
                recv_sem=recv.at[step],
                device_id=device,
                device_id_type=MESH,
            )

        def start(step, carry):
            copy(step).start()
            return carry

        def finish(step, carry):
            copy(step).wait()
            return carry

        lax.fori_loop(1, count, start, 0)
        own = pltpu.make_async_copy(source(mine), target(mine), local.at[slot])
        own.start()
        own.wait()
        lax.fori_loop(1, count, finish, 0)

    given = scan_ref[...].reshape(LANES, ROWS)
    parts = [given[:, b * 128 : (b + 1) * 128] for b in range(4)]
    flipped = dot(jnp.concatenate(parts, axis=0), swap_matrix)
    backward = jnp.concatenate(
        [flipped[(3 - b) * 128 : (4 - b) * 128].T for b in range(4)], axis=0
    )
    forward = jnp.concatenate([part.T for part in parts], axis=0)
    ordered = jnp.where(upper, pltpu.roll(backward, 1, 0), forward)
    rows[...] = ordered.reshape(LINE, PLANE, LANES)

    exchange(
        LINE, line_peer, lambda p: rows.at[p], lambda m: mid.at[m], line,
        send_line, recv_line, 0,
    )
    exchange(
        PLANE, plane_peer, lambda p: mid.at[:, p], lambda m: landed.at[m], plane,
        send_plane, recv_plane, 1,
    )

    blocks = [
        landed[16 * (n // 2) : 16 * (n // 2) + 16, 8 * (n % 2) : 8 * (n % 2) + 8, :].reshape(
            128, LANES
        )
        for n in range(4)
    ]
    first_device = line + plane == 0
    outcome = correlate(blocks, first_device, big_ref, square_ref, pltpu.roll)
    for n in range(4):
        result[16 * (n // 2) : 16 * (n // 2) + 16, 8 * (n % 2) : 8 * (n % 2) + 8, :] = outcome[
            n
        ].reshape(16, 8, LANES)

    exchange(
        PLANE, plane_peer, lambda p: result.at[p], lambda m: mid_back.at[m], plane,
        send_plane_back, recv_plane_back, 2,
    )
    exchange(
        LINE, line_peer, lambda p: mid_back.at[:, p], lambda m: landed_back.at[m], line,
        send_line_back, recv_line_back, 3,
    )

    ordered = landed_back[...].reshape(ROWS, LANES)
    turned = dot(
        swap_matrix,
        jnp.concatenate([ordered[b * 128 : (b + 1) * 128] for b in (3, 2, 1, 0)], axis=1),
    )
    backward = jnp.concatenate([turned[:, b * 128 : (b + 1) * 128] for b in range(4)], axis=0)
    ordered = jnp.where(upper, pltpu.roll(backward, 1, 0), ordered)
    final = jnp.concatenate([ordered[b * 128 : (b + 1) * 128].T for b in range(4)], axis=1)
    out_ref[...] = final.reshape(out_ref.shape)


def on_device(scan_pair, big, squares):
    vmem = pl.BlockSpec(memory_space=pltpu.VMEM)
    dma = pltpu.SemaphoreType.DMA
    return pl.pallas_call(
        kernel,
        out_shape=jax.ShapeDtypeStruct(scan_pair.shape, jnp.float32),
        in_specs=[vmem] * 3,
        out_specs=vmem,
        scratch_shapes=[
            pltpu.VMEM((LINE, PLANE, LANES), jnp.float32),
            pltpu.VMEM((LINE, PLANE, LANES), jnp.float32),
            pltpu.VMEM((PLANE, LINE, LANES), jnp.float32),
            pltpu.VMEM((PLANE, LINE, LANES), jnp.float32),
            pltpu.VMEM((PLANE, LINE, LANES), jnp.float32),
            pltpu.VMEM((LINE, PLANE, LANES), jnp.float32),
            dma((LINE,)), dma((LINE,)), dma((PLANE,)), dma((PLANE,)),
            dma((PLANE,)), dma((PLANE,)), dma((LINE,)), dma((LINE,)), dma((4,)),
        ],
        compiler_params=pltpu.CompilerParams(has_side_effects=True),
    )(scan_pair, big, squares)


def solution(mesh):
    big, squares = constants()

    def body(scan_pair):
        return on_device(scan_pair, jnp.asarray(big), jnp.asarray(squares))

    return jax.shard_map(
        body,
        mesh=mesh,
        in_specs=(P(None, None, "wide", "narrow"),),
        out_specs=P(None, None, "wide", "narrow"),
        check_vma=False,
    )
```

```python
import functools
import math

import jax
import jax.numpy as jnp
import numpy as np
from jax import lax
from jax.experimental import pallas as pl
from jax.experimental.pallas import tpu as pltpu
from jax.sharding import PartitionSpec as P

magnitude_floor = 0.25
MESH = pl.DeviceIdType.MESH

LINE, PLANE, LANES, ROWS = 16, 32, 128, 512
LENGTH, POINTS = 2048, 16


def constants():
    ka = np.arange(128)
    j = np.arange(128)
    z1 = (j % 8) * 16 + j // 8
    big = np.exp(-2j * np.pi * ((ka[:, None] * z1[None, :]) % 128) / 128)
    forward_big = np.concatenate([big.real, big.imag], axis=0)
    back = np.conj(big).T
    inverse_big = np.concatenate([back.real, back.imag], axis=0)

    z0 = np.arange(POINTS)
    small = np.exp(-2j * np.pi * ((z0[:, None] * z0[None, :]) % POINTS) / POINTS) / math.sqrt(LENGTH)

    def lanes(matrix, columns):
        block = np.einsum("xw,zk->xzwk", columns, matrix).reshape(64, 64)
        return np.block([[block.real, block.imag], [-block.imag, block.real]])

    same, reverse = np.eye(4), np.eye(4)[::-1]
    turn = np.exp(-2j * np.pi * ka[:, None] * z0[None, :] / LENGTH)
    turn = np.tile(turn, (1, 4))
    turn_real = np.concatenate([turn.real, turn.real], axis=1)
    turn_imag = np.concatenate([-turn.imag, turn.imag], axis=1)
    squares = np.stack(
        [
            lanes(small, same),
            lanes(small, reverse),
            lanes(np.conj(small), same),
            turn_real,
            turn_imag,
            np.eye(128)[::-1],
        ]
    )
    return (
        np.stack([forward_big, inverse_big]).astype(np.float32),
        squares.astype(np.float32),
    )


def dot(left, right):
    return jnp.dot(
        left, right, precision=lax.Precision.HIGHEST, preferred_element_type=jnp.float32
    )


def correlate(blocks, first_device, big_ref, square_ref, roll):
    def swap(value):
        return roll(value, 64, 1)

    lane = lax.broadcasted_iota(jnp.int32, (128, LANES), 1)
    real_lane = lane < 64
    sign = jnp.where(real_lane, -1.0, 1.0).astype(jnp.float32)
    turn_real, turn_imag = square_ref[3], square_ref[4]

    both = dot(big_ref[0], jnp.concatenate(blocks, axis=1))
    own, twin = [], []
    for n in range(4):
        upper = both[:128, n * 128 : (n + 1) * 128]
        lower = swap(both[128:, n * 128 : (n + 1) * 128])
        straight = upper + sign * lower
        conjugate = lower - sign * upper
        own.append(straight * turn_real + swap(straight) * turn_imag)
        twin.append(conjugate * turn_real + swap(conjugate) * turn_imag)
    mirrored = [
        jnp.where(first_device, twin[a], twin[b]) for a, b in ((0, 3), (3, 2), (2, 1), (1, 0))
    ]
    spectrum = dot(jnp.concatenate(own, axis=0), square_ref[0])
    mirror_spectrum = dot(jnp.concatenate(mirrored, axis=0), square_ref[1])
    normalized = []
    for n in range(4):
        s = spectrum[n * 128 : (n + 1) * 128]
        m = mirror_spectrum[n * 128 : (n + 1) * 128]
        first = (s + m) * 0.5
        half = (s - m) * 0.5
        turned = first * swap(half)
        plain = first * half
        cross = jnp.where(real_lane, turned - swap(turned), plain + swap(plain))
        square = cross * cross
        modulus = jnp.maximum(jnp.sqrt(square + swap(square)), magnitude_floor)
        normalized.append(cross / modulus)
    back = dot(jnp.concatenate(normalized, axis=0), square_ref[2])
    turned_back = []
    for n in range(4):
        value = back[n * 128 : (n + 1) * 128]
        turned_back.append(value * turn_real - swap(value) * turn_imag)
    both = dot(big_ref[1], jnp.concatenate(turned_back, axis=1))
    return [
        both[:128, n * 128 : (n + 1) * 128] + sign * swap(both[128:, n * 128 : (n + 1) * 128])
        for n in range(4)
    ]


def kernel(
    scan_ref, big_ref, square_ref, out_ref,
    rows, mid, landed, result, mid_back, landed_back,
    send_line, recv_line, send_plane, recv_plane,
    send_plane_back, recv_plane_back, send_line_back, recv_line_back, local,
):
    narrow, wide = lax.axis_index("narrow"), lax.axis_index("wide")
    y_hi, core = narrow // 2, narrow % 2
    z, sheet = wide // 16, wide % 16
    line = core * 8 + z
    plane = y_hi * 16 + sheet
    upper = narrow >= 2
    swap_matrix = square_ref[5]

    def line_peer(step):
        peer = (line + step) % LINE
        return peer, (y_hi * 2 + peer // 8, (peer % 8) * 16 + sheet)

    def plane_peer(step):
        peer = (plane + step) % PLANE
        return peer, ((peer // 16) * 2 + core, z * 16 + peer % 16)

    def exchange(count, peer_of, source, target, mine, send, recv, slot):
        def copy(step):
            peer, device = peer_of(step)
            return pltpu.make_async_remote_copy(
                src_ref=source(peer),
                dst_ref=target(mine),
                send_sem=send.at[step],
                recv_sem=recv.at[step],
                device_id=device,
                device_id_type=MESH,
            )

        def start(step, carry):
            copy(step).start()
            return carry

        def finish(step, carry):
            copy(step).wait()
            return carry

        lax.fori_loop(1, count, start, 0)
        own = pltpu.make_async_copy(source(mine), target(mine), local.at[slot])
        own.start()
        own.wait()
        lax.fori_loop(1, count, finish, 0)

    barrier = pltpu.get_barrier_semaphore()

    def greet(peer_of):
        def signal(step, carry):
            pl.semaphore_signal(
                barrier, inc=1, device_id=peer_of(step)[1], device_id_type=MESH
            )
            return carry

        return signal

    lax.fori_loop(1, PLANE, greet(plane_peer), 0)
    lax.fori_loop(1, LINE, greet(line_peer), 0)

    given = scan_ref[...].reshape(LANES, ROWS)
    parts = [given[:, b * 128 : (b + 1) * 128] for b in range(4)]
    flipped = dot(jnp.concatenate(parts, axis=0), swap_matrix)
    backward = jnp.concatenate(
        [flipped[(3 - b) * 128 : (4 - b) * 128].T for b in range(4)], axis=0
    )
    forward = jnp.concatenate([part.T for part in parts], axis=0)
    ordered = jnp.where(upper, pltpu.roll(backward, 1, 0), forward)
    rows[...] = ordered.reshape(LINE, PLANE, LANES)
    pl.semaphore_wait(barrier, LINE + PLANE - 2)

    exchange(
        LINE, line_peer, lambda p: rows.at[p], lambda m: mid.at[m], line,
        send_line, recv_line, 0,
    )
    exchange(
        PLANE, plane_peer, lambda p: mid.at[:, p], lambda m: landed.at[m], plane,
        send_plane, recv_plane, 1,
    )

    blocks = [
        landed[16 * (n // 2) : 16 * (n // 2) + 16, 8 * (n % 2) : 8 * (n % 2) + 8, :].reshape(
            128, LANES
        )
        for n in range(4)
    ]
    first_device = line + plane == 0
    outcome = correlate(blocks, first_device, big_ref, square_ref, pltpu.roll)
    for n in range(4):
        result[16 * (n // 2) : 16 * (n // 2) + 16, 8 * (n % 2) : 8 * (n % 2) + 8, :] = outcome[
            n
        ].reshape(16, 8, LANES)

    exchange(
        PLANE, plane_peer, lambda p: result.at[p], lambda m: mid_back.at[m], plane,
        send_plane_back, recv_plane_back, 2,
    )
    exchange(
        LINE, line_peer, lambda p: mid_back.at[:, p], lambda m: landed_back.at[m], line,
        send_line_back, recv_line_back, 3,
    )

    ordered = landed_back[...].reshape(ROWS, LANES)
    turned = dot(
        swap_matrix,
        jnp.concatenate([ordered[b * 128 : (b + 1) * 128] for b in (3, 2, 1, 0)], axis=1),
    )
    backward = jnp.concatenate([turned[:, b * 128 : (b + 1) * 128] for b in range(4)], axis=0)
    ordered = jnp.where(upper, pltpu.roll(backward, 1, 0), ordered)
    final = jnp.concatenate([ordered[b * 128 : (b + 1) * 128].T for b in range(4)], axis=1)
    out_ref[...] = final.reshape(out_ref.shape)


def on_device(scan_pair, big, squares):
    vmem = pl.BlockSpec(memory_space=pltpu.VMEM)
    dma = pltpu.SemaphoreType.DMA
    return pl.pallas_call(
        kernel,
        out_shape=jax.ShapeDtypeStruct(scan_pair.shape, jnp.float32),
        in_specs=[vmem] * 3,
        out_specs=vmem,
        scratch_shapes=[
            pltpu.VMEM((LINE, PLANE, LANES), jnp.float32),
            pltpu.VMEM((LINE, PLANE, LANES), jnp.float32),
            pltpu.VMEM((PLANE, LINE, LANES), jnp.float32),
            pltpu.VMEM((PLANE, LINE, LANES), jnp.float32),
            pltpu.VMEM((PLANE, LINE, LANES), jnp.float32),
            pltpu.VMEM((LINE, PLANE, LANES), jnp.float32),
            dma((LINE,)), dma((LINE,)), dma((PLANE,)), dma((PLANE,)),
            dma((PLANE,)), dma((PLANE,)), dma((LINE,)), dma((LINE,)), dma((4,)),
        ],
        compiler_params=pltpu.CompilerParams(collective_id=0, has_side_effects=True),
    )(scan_pair, big, squares)


def solution(mesh):
    big, squares = constants()

    def body(scan_pair):
        return on_device(scan_pair, jnp.asarray(big), jnp.asarray(squares))

    return jax.shard_map(
        body,
        mesh=mesh,
        in_specs=(P(None, None, "wide", "narrow"),),
        out_specs=P(None, None, "wide", "narrow"),
        check_vma=False,
    )
```

```python
import functools
import math

import jax
import jax.numpy as jnp
import numpy as np
from jax import lax
from jax.experimental import pallas as pl
from jax.experimental.pallas import tpu as pltpu
from jax.sharding import PartitionSpec as P

magnitude_floor = 0.25
MESH = pl.DeviceIdType.MESH

LINE, PLANE, LANES, ROWS = 16, 32, 128, 512
LENGTH, POINTS = 2048, 16


def constants():
    ka = np.arange(128)
    j = np.arange(128)
    z1 = (j % 8) * 16 + j // 8
    big = np.exp(-2j * np.pi * ((ka[:, None] * z1[None, :]) % 128) / 128)
    forward_big = np.concatenate([big.real, big.imag], axis=0)
    back = np.conj(big).T
    inverse_big = np.concatenate([back.real, back.imag], axis=0)

    z0 = np.arange(POINTS)
    small = np.exp(-2j * np.pi * ((z0[:, None] * z0[None, :]) % POINTS) / POINTS) / math.sqrt(LENGTH)

    def lanes(matrix, columns):
        block = np.einsum("xw,zk->xzwk", columns, matrix).reshape(64, 64)
        return np.block([[block.real, block.imag], [-block.imag, block.real]])

    same, reverse = np.eye(4), np.eye(4)[::-1]
    turn = np.exp(-2j * np.pi * ka[:, None] * z0[None, :] / LENGTH)
    turn = np.tile(turn, (1, 4))
    turn_real = np.concatenate([turn.real, turn.real], axis=1)
    turn_imag = np.concatenate([-turn.imag, turn.imag], axis=1)
    squares = np.stack(
        [
            lanes(small, same),
            lanes(small, reverse),
            lanes(np.conj(small), same),
            turn_real,
            turn_imag,
            np.eye(128)[::-1],
        ]
    )
    return (
        np.stack([forward_big, inverse_big]).astype(np.float32),
        squares.astype(np.float32),
    )


def dot(left, right):
    return jnp.dot(
        left, right, precision=lax.Precision.HIGHEST, preferred_element_type=jnp.float32
    )


def correlate(blocks, first_device, big_ref, square_ref, roll):
    def swap(value):
        return roll(value, 64, 1)

    lane = lax.broadcasted_iota(jnp.int32, (128, LANES), 1)
    real_lane = lane < 64
    sign = jnp.where(real_lane, -1.0, 1.0).astype(jnp.float32)
    turn_real, turn_imag = square_ref[3], square_ref[4]

    both = dot(big_ref[0], jnp.concatenate(blocks, axis=1))
    own, twin = [], []
    for n in range(4):
        upper = both[:128, n * 128 : (n + 1) * 128]
        lower = swap(both[128:, n * 128 : (n + 1) * 128])
        straight = upper + sign * lower
        conjugate = lower - sign * upper
        own.append(straight * turn_real + swap(straight) * turn_imag)
        twin.append(conjugate * turn_real + swap(conjugate) * turn_imag)
    mirrored = [
        jnp.where(first_device, twin[a], twin[b]) for a, b in ((0, 3), (3, 2), (2, 1), (1, 0))
    ]
    spectrum = dot(jnp.concatenate(own, axis=0), square_ref[0])
    mirror_spectrum = dot(jnp.concatenate(mirrored, axis=0), square_ref[1])
    normalized = []
    for n in range(4):
        s = spectrum[n * 128 : (n + 1) * 128]
        m = mirror_spectrum[n * 128 : (n + 1) * 128]
        first = (s + m) * 0.5
        half = (s - m) * 0.5
        turned = first * swap(half)
        plain = first * half
        cross = jnp.where(real_lane, turned - swap(turned), plain + swap(plain))
        square = cross * cross
        modulus = jnp.maximum(jnp.sqrt(square + swap(square)), magnitude_floor)
        normalized.append(cross / modulus)
    back = dot(jnp.concatenate(normalized, axis=0), square_ref[2])
    turned_back = []
    for n in range(4):
        value = back[n * 128 : (n + 1) * 128]
        turned_back.append(value * turn_real - swap(value) * turn_imag)
    both = dot(big_ref[1], jnp.concatenate(turned_back, axis=1))
    return [
        both[:128, n * 128 : (n + 1) * 128] + sign * swap(both[128:, n * 128 : (n + 1) * 128])
        for n in range(4)
    ]


def kernel(
    scan_ref, big_ref, square_ref, out_ref,
    rows, mid, landed, result, paired, arrived,
    send_line, recv_line, send_plane, recv_plane,
    send_core, recv_core, send_back, recv_back, local,
):
    narrow, wide = lax.axis_index("narrow"), lax.axis_index("wide")
    y_hi, core = narrow // 2, narrow % 2
    z, sheet = wide // 16, wide % 16
    line = core * 8 + z
    plane = y_hi * 16 + sheet
    upper = narrow >= 2
    swap_matrix = square_ref[5]

    def line_peer(step):
        peer = (line + step) % LINE
        return peer, (y_hi * 2 + peer // 8, (peer % 8) * 16 + sheet)

    def plane_peer(step):
        peer = (plane + step) % PLANE
        return peer, ((peer // 16) * 2 + core, z * 16 + peer % 16)

    def exchange(count, peer_of, source, target, mine, send, recv, slot):
        def copy(step):
            peer, device = peer_of(step)
            return pltpu.make_async_remote_copy(
                src_ref=source(peer),
                dst_ref=target(mine),
                send_sem=send.at[step],
                recv_sem=recv.at[step],
                device_id=device,
                device_id_type=MESH,
            )

        def start(step, carry):
            copy(step).start()
            return carry

        def finish(step, carry):
            copy(step).wait()
            return carry

        lax.fori_loop(1, count, start, 0)
        own = pltpu.make_async_copy(source(mine), target(mine), local.at[slot])
        own.start()
        own.wait()
        lax.fori_loop(1, count, finish, 0)

    barrier = pltpu.get_barrier_semaphore()

    def greet(peer_of):
        def signal(step, carry):
            pl.semaphore_signal(
                barrier, inc=1, device_id=peer_of(step)[1], device_id_type=MESH
            )
            return carry

        return signal

    lax.fori_loop(1, PLANE, greet(plane_peer), 0)
    lax.fori_loop(1, LINE, greet(line_peer), 0)

    given = scan_ref[...].reshape(LANES, ROWS)
    parts = [given[:, b * 128 : (b + 1) * 128] for b in range(4)]

    @pl.when(upper)
    def _():
        flipped = dot(jnp.concatenate(parts, axis=0), swap_matrix)
        backward = jnp.concatenate(
            [flipped[(3 - b) * 128 : (4 - b) * 128].T for b in range(4)], axis=0
        )
        rows[...] = pltpu.roll(backward, 1, 0).reshape(LINE, PLANE, LANES)

    @pl.when(jnp.logical_not(upper))
    def _():
        forward = jnp.concatenate([part.T for part in parts], axis=0)
        rows[...] = forward.reshape(LINE, PLANE, LANES)

    pl.semaphore_wait(barrier, LINE + PLANE - 2)

    exchange(
        LINE, line_peer, lambda p: rows.at[p], lambda m: mid.at[m], line,
        send_line, recv_line, 0,
    )
    exchange(
        PLANE, plane_peer, lambda p: mid.at[:, p], lambda m: landed.at[m], plane,
        send_plane, recv_plane, 1,
    )

    blocks = [
        landed[16 * (n // 2) : 16 * (n // 2) + 16, 8 * (n % 2) : 8 * (n % 2) + 8, :].reshape(
            128, LANES
        )
        for n in range(4)
    ]
    first_device = line + plane == 0
    outcome = correlate(blocks, first_device, big_ref, square_ref, pltpu.roll)
    for n in range(4):
        result[n % 2, (n // 2) * 128 : (n // 2) * 128 + 128, :] = outcome[n]

    place = z * 32 + plane
    place_mirror = (256 - place) % 256
    other = 1 - core
    slots = (core, jnp.where(place == 0, core, other))
    partner = (y_hi * 2 + other, wide)

    def half(half_index):
        return pl.ds(half_index * 128, 128)

    swaps = [
        pltpu.make_async_remote_copy(
            src_ref=result.at[other, half(h)],
            dst_ref=paired.at[slots[h], half(h)],
            send_sem=send_core.at[h],
            recv_sem=recv_core.at[h],
            device_id=partner,
            device_id_type=MESH,
        )
        for h in range(2)
    ]
    keeps = [
        pltpu.make_async_copy(
            result.at[core, half(h)], paired.at[slots[h], half(h)], local.at[2 + h]
        )
        for h in range(2)
    ]
    for copy in swaps + keeps:
        copy.start()
    for copy in swaps + keeps:
        copy.wait()

    x, y = sheet // 4, y_hi * 4 + sheet % 4
    for far_x in (2, 1, 3, 0):
        to_x = (x + far_x) % 4

        def row_of_chips(step, carry, to_x=to_x, far_x=far_x):
            bend = (step + 1) // 2
            to_y = (y + 4 + jnp.where(step % 2 == 1, -bend, bend)) % 8
            to_half, to_sheet = to_y // 4, to_x * 4 + to_y % 4
            to_place = jnp.where(to_half == 0, place, place_mirror)
            for far_z in (4, 3, 5, 2, 6, 1, 7, 0):
                to_z = (z + far_z) % 8
                copy = pltpu.make_async_remote_copy(
                    src_ref=paired.at[:, (to_half * 16 + to_sheet) * 8 + to_z],
                    dst_ref=arrived.at[:, to_place],
                    send_sem=send_back.at[0],
                    recv_sem=recv_back.at[0],
                    device_id=(to_half * 2 + core, to_z * 16 + to_sheet),
                    device_id_type=MESH,
                )
                if far_x == 0 and far_z == 0:
                    pl.when(step < 7)(copy.start)
                else:
                    copy.start()
            return carry

        lax.fori_loop(0, 8, row_of_chips, 0)
    own = pltpu.make_async_copy(
        paired.at[:, plane_row(y_hi, sheet, z)],
        arrived.at[:, jnp.where(y_hi == 0, place, place_mirror)],
        local.at[4],
    )
    own.start()
    own.wait()
    everything = arrived.at[:, pl.ds(0, 255)]
    pltpu.make_async_copy(everything, everything, send_back.at[0]).wait()
    pltpu.make_async_copy(everything, everything, recv_back.at[0]).wait()
    out_ref[...] = arrived[...].reshape(ROWS, LANES)


def plane_row(y_hi, sheet, z):
    return (y_hi * 16 + sheet) * 8 + z


def turn_kernel(rows_ref, out_ref):
    rows = rows_ref[...]
    final = jnp.concatenate([rows[b * 128 : (b + 1) * 128].T for b in range(4)], axis=1)
    out_ref[...] = final.reshape(out_ref.shape)


def on_device(scan_pair, big, squares):
    vmem = pl.BlockSpec(memory_space=pltpu.VMEM)
    dma = pltpu.SemaphoreType.DMA
    exchanged = pl.pallas_call(
        kernel,
        out_shape=jax.ShapeDtypeStruct((ROWS, LANES), jnp.float32),
        in_specs=[vmem] * 3,
        out_specs=vmem,
        scratch_shapes=[
            pltpu.VMEM((LINE, PLANE, LANES), jnp.float32),
            pltpu.VMEM((LINE, PLANE, LANES), jnp.float32),
            pltpu.VMEM((PLANE, LINE, LANES), jnp.float32),
            pltpu.VMEM((2, 256, LANES), jnp.float32),
            pltpu.VMEM((2, 256, LANES), jnp.float32),
            pltpu.VMEM((2, 256, LANES), jnp.float32),
            dma((LINE,)), dma((LINE,)), dma((PLANE,)), dma((PLANE,)),
            dma((2,)), dma((2,)), dma((1,)), dma((1,)), dma((5,)),
        ],
        compiler_params=pltpu.CompilerParams(collective_id=0, has_side_effects=True),
    )(scan_pair, big, squares)
    return pl.pallas_call(
        turn_kernel,
        out_shape=jax.ShapeDtypeStruct(scan_pair.shape, jnp.float32),
        in_specs=[vmem],
        out_specs=vmem,
    )(exchanged)


def solution(mesh):
    big, squares = constants()

    def body(scan_pair):
        return on_device(scan_pair, jnp.asarray(big), jnp.asarray(squares))

    return jax.shard_map(
        body,
        mesh=mesh,
        in_specs=(P(None, None, "wide", "narrow"),),
        out_specs=P(None, None, "wide", "narrow"),
        check_vma=False,
    )
```

```python
import functools
import math

import jax
import jax.numpy as jnp
import numpy as np
from jax import lax
from jax.experimental import pallas as pl
from jax.experimental.pallas import tpu as pltpu
from jax.sharding import PartitionSpec as P

magnitude_floor = 0.25
MESH = pl.DeviceIdType.MESH

LINE, PLANE, LANES, ROWS = 16, 32, 128, 512
LENGTH, POINTS = 2048, 16


def constants():
    ka = np.arange(128)
    j = np.arange(128)
    z1 = (j % 8) * 16 + j // 8
    big = np.exp(-2j * np.pi * ((ka[:, None] * z1[None, :]) % 128) / 128)
    forward_big = np.concatenate([big.real, big.imag], axis=0)
    back = np.conj(big).T
    inverse_big = np.concatenate([back.real, back.imag], axis=0)

    z0 = np.arange(POINTS)
    small = np.exp(-2j * np.pi * ((z0[:, None] * z0[None, :]) % POINTS) / POINTS) / math.sqrt(LENGTH)

    def lanes(matrix, columns):
        block = np.einsum("xw,zk->xzwk", columns, matrix).reshape(64, 64)
        return np.block([[block.real, block.imag], [-block.imag, block.real]])

    same, reverse = np.eye(4), np.eye(4)[::-1]
    turn = np.exp(-2j * np.pi * ka[:, None] * z0[None, :] / LENGTH)
    turn = np.tile(turn, (1, 4))
    turn_real = np.concatenate([turn.real, turn.real], axis=1)
    turn_imag = np.concatenate([-turn.imag, turn.imag], axis=1)
    squares = np.stack(
        [
            lanes(small, same),
            lanes(small, reverse),
            lanes(np.conj(small), same),
            turn_real,
            turn_imag,
            np.eye(128)[::-1],
        ]
    )
    return (
        np.stack([forward_big, inverse_big]).astype(np.float32),
        squares.astype(np.float32),
    )


def dot(left, right):
    return jnp.dot(
        left, right, precision=lax.Precision.HIGHEST, preferred_element_type=jnp.float32
    )


def correlate(blocks, first_device, big_ref, square_ref, roll):
    def swap(value):
        return roll(value, 64, 1)

    lane = lax.broadcasted_iota(jnp.int32, (128, LANES), 1)
    real_lane = lane < 64
    sign = jnp.where(real_lane, -1.0, 1.0).astype(jnp.float32)
    turn_real, turn_imag = square_ref[3], square_ref[4]

    both = dot(big_ref[0], jnp.concatenate(blocks, axis=1))
    own, twin = [], []
    for n in range(4):
        upper = both[:128, n * 128 : (n + 1) * 128]
        lower = swap(both[128:, n * 128 : (n + 1) * 128])
        straight = upper + sign * lower
        conjugate = lower - sign * upper
        own.append(straight * turn_real + swap(straight) * turn_imag)
        twin.append(conjugate * turn_real + swap(conjugate) * turn_imag)
    mirrored = [
        jnp.where(first_device, twin[a], twin[b]) for a, b in ((0, 3), (3, 2), (2, 1), (1, 0))
    ]
    spectrum = dot(jnp.concatenate(own, axis=0), square_ref[0])
    mirror_spectrum = dot(jnp.concatenate(mirrored, axis=0), square_ref[1])
    normalized = []
    for n in range(4):
        s = spectrum[n * 128 : (n + 1) * 128]
        m = mirror_spectrum[n * 128 : (n + 1) * 128]
        first = (s + m) * 0.5
        half = (s - m) * 0.5
        turned = first * swap(half)
        plain = first * half
        cross = jnp.where(real_lane, turned - swap(turned), plain + swap(plain))
        square = cross * cross
        modulus = jnp.maximum(jnp.sqrt(square + swap(square)), magnitude_floor)
        normalized.append(cross / modulus)
    back = dot(jnp.concatenate(normalized, axis=0), square_ref[2])
    turned_back = []
    for n in range(4):
        value = back[n * 128 : (n + 1) * 128]
        turned_back.append(value * turn_real - swap(value) * turn_imag)
    both = dot(big_ref[1], jnp.concatenate(turned_back, axis=1))
    return [
        both[:128, n * 128 : (n + 1) * 128] + sign * swap(both[128:, n * 128 : (n + 1) * 128])
        for n in range(4)
    ]


def kernel(
    scan_ref, big_ref, square_ref, out_ref,
    rows, mid, landed, result, paired, arrived,
    send_line, recv_line, send_plane, recv_plane,
    send_core, recv_core, send_back, recv_back, local,
):
    narrow, wide = lax.axis_index("narrow"), lax.axis_index("wide")
    y_hi, core = narrow // 2, narrow % 2
    z, sheet = wide // 16, wide % 16
    line = core * 8 + z
    x, y = sheet // 4, y_hi * 4 + sheet % 4
    plane = x * 8 + y
    upper = narrow >= 2
    swap_matrix = square_ref[5]

    def line_peer(step):
        peer = (line + step) % LINE
        return peer, (y_hi * 2 + peer // 8, (peer % 8) * 16 + sheet)

    def plane_peer(step):
        to_x, to_y = (x + step // 8) % 4, (y + step) % 8
        return to_x * 8 + to_y, ((to_y // 4) * 2 + core, z * 16 + to_x * 4 + to_y % 4)

    def line_copy(far_x, step):
        peer, device = line_peer(step)
        first = pl.multiple_of(((x + far_x) % 4) * 8, 8)
        return pltpu.make_async_remote_copy(
            src_ref=rows.at[peer, pl.ds(first, 8)],
            dst_ref=mid.at[line, pl.ds(first, 8)],
            send_sem=send_line.at[far_x, step],
            recv_sem=recv_line.at[far_x, step],
            device_id=device,
            device_id_type=MESH,
        )

    def plane_copy(step):
        peer, device = plane_peer(step)
        return pltpu.make_async_remote_copy(
            src_ref=mid.at[:, peer],
            dst_ref=landed.at[x, y],
            send_sem=send_plane.at[step],
            recv_sem=recv_plane.at[step],
            device_id=device,
            device_id_type=MESH,
        )

    def each(low, high, act):
        def body(step, carry):
            act(step)
            return carry

        lax.fori_loop(low, high, body, 0)

    barrier = pltpu.get_barrier_semaphore()

    def greet(peer_of):
        def signal(step, carry):
            pl.semaphore_signal(
                barrier, inc=1, device_id=peer_of(step)[1], device_id_type=MESH
            )
            return carry

        return signal

    lax.fori_loop(1, PLANE, greet(plane_peer), 0)
    lax.fori_loop(1, LINE, greet(line_peer), 0)

    given = scan_ref[...].reshape(LANES, ROWS)
    parts = [given[:, b * 128 : (b + 1) * 128] for b in range(4)]

    @pl.when(upper)
    def _():
        flipped = dot(jnp.concatenate(parts, axis=0), swap_matrix)
        backward = jnp.concatenate(
            [flipped[(3 - b) * 128 : (4 - b) * 128].T for b in range(4)], axis=0
        )
        rows[...] = pltpu.roll(backward, 1, 0).reshape(LINE, PLANE, LANES)

    @pl.when(jnp.logical_not(upper))
    def _():
        forward = jnp.concatenate([part.T for part in parts], axis=0)
        rows[...] = forward.reshape(LINE, PLANE, LANES)

    pl.semaphore_wait(barrier, LINE + PLANE - 2)

    parts_order = (2, 1, 3, 0)
    for far_x in parts_order:
        each(1, LINE, lambda step: line_copy(far_x, step).start())
    own = pltpu.make_async_copy(rows.at[line], mid.at[line], local.at[0])
    own.start()
    own.wait()
    for far_x in parts_order:
        each(1, LINE, lambda step: line_copy(far_x, step).wait_recv())
        each(max(far_x * 8, 1), far_x * 8 + 8, lambda step: plane_copy(step).start())
    own = pltpu.make_async_copy(mid.at[:, plane], landed.at[x, y], local.at[1])
    own.start()
    own.wait()
    for far_x in parts_order:
        each(1, LINE, lambda step: line_copy(far_x, step).wait_send())
    each(1, PLANE, lambda step: plane_copy(step).wait())

    blocks = [
        landed[
            :, 4 * (n // 2) : 4 * (n // 2) + 4, 8 * (n % 2) : 8 * (n % 2) + 8, :
        ].reshape(128, LANES)
        for n in range(4)
    ]
    first_device = line + plane == 0
    outcome = correlate(blocks, first_device, big_ref, square_ref, pltpu.roll)
    for n in range(4):
        result[n % 2, (n // 2) * 128 : (n // 2) * 128 + 128, :] = outcome[n]

    place = z * 32 + plane
    place_mirror = (256 - place) % 256
    other = 1 - core
    slots = (core, jnp.where(place == 0, core, other))
    partner = (y_hi * 2 + other, wide)

    def half(half_index):
        return pl.ds(half_index * 128, 128)

    swaps = [
        pltpu.make_async_remote_copy(
            src_ref=result.at[other, half(h)],
            dst_ref=paired.at[slots[h], half(h)],
            send_sem=send_core.at[h],
            recv_sem=recv_core.at[h],
            device_id=partner,
            device_id_type=MESH,
        )
        for h in range(2)
    ]
    keeps = [
        pltpu.make_async_copy(
            result.at[core, half(h)], paired.at[slots[h], half(h)], local.at[2 + h]
        )
        for h in range(2)
    ]
    for copy in swaps + keeps:
        copy.start()
    for copy in swaps + keeps:
        copy.wait()

    for far_x in (2, 1, 3, 0):
        to_x = (x + far_x) % 4

        def row_of_chips(step, carry, to_x=to_x, far_x=far_x):
            bend = (step + 1) // 2
            to_y = (y + 4 + jnp.where(step % 2 == 1, -bend, bend)) % 8
            to_half, to_sheet = to_y // 4, to_x * 4 + to_y % 4
            to_place = jnp.where(to_half == 0, place, place_mirror)
            for far_z in (4, 3, 5, 2, 6, 1, 7, 0):
                to_z = (z + far_z) % 8
                copy = pltpu.make_async_remote_copy(
                    src_ref=paired.at[:, (to_half * 16 + to_sheet) * 8 + to_z],
                    dst_ref=arrived.at[:, to_place],
                    send_sem=send_back.at[0],
                    recv_sem=recv_back.at[0],
                    device_id=(to_half * 2 + core, to_z * 16 + to_sheet),
                    device_id_type=MESH,
                )
                if far_x == 0 and far_z == 0:
                    pl.when(step < 7)(copy.start)
                else:
                    copy.start()
            return carry

        lax.fori_loop(0, 8, row_of_chips, 0)
    own = pltpu.make_async_copy(
        paired.at[:, plane_row(y_hi, sheet, z)],
        arrived.at[:, jnp.where(y_hi == 0, place, place_mirror)],
        local.at[4],
    )
    own.start()
    own.wait()
    everything = arrived.at[:, pl.ds(0, 255)]
    pltpu.make_async_copy(everything, everything, send_back.at[0]).wait()
    pltpu.make_async_copy(everything, everything, recv_back.at[0]).wait()
    out_ref[...] = arrived[...].reshape(ROWS, LANES)


def plane_row(y_hi, sheet, z):
    return (y_hi * 16 + sheet) * 8 + z


def turn_kernel(rows_ref, out_ref):
    rows = rows_ref[...]
    final = jnp.concatenate([rows[b * 128 : (b + 1) * 128].T for b in range(4)], axis=1)
    out_ref[...] = final.reshape(out_ref.shape)


def on_device(scan_pair, big, squares):
    vmem = pl.BlockSpec(memory_space=pltpu.VMEM)
    dma = pltpu.SemaphoreType.DMA
    exchanged = pl.pallas_call(
        kernel,
        out_shape=jax.ShapeDtypeStruct((ROWS, LANES), jnp.float32),
        in_specs=[vmem] * 3,
        out_specs=vmem,
        scratch_shapes=[
            pltpu.VMEM((LINE, PLANE, LANES), jnp.float32),
            pltpu.VMEM((LINE, PLANE, LANES), jnp.float32),
            pltpu.VMEM((4, 8, LINE, LANES), jnp.float32),
            pltpu.VMEM((2, 256, LANES), jnp.float32),
            pltpu.VMEM((2, 256, LANES), jnp.float32),
            pltpu.VMEM((2, 256, LANES), jnp.float32),
            dma((4, LINE)), dma((4, LINE)), dma((PLANE,)), dma((PLANE,)),
            dma((2,)), dma((2,)), dma((1,)), dma((1,)), dma((5,)),
        ],
        compiler_params=pltpu.CompilerParams(collective_id=0, has_side_effects=True),
    )(scan_pair, big, squares)
    return pl.pallas_call(
        turn_kernel,
        out_shape=jax.ShapeDtypeStruct(scan_pair.shape, jnp.float32),
        in_specs=[vmem],
        out_specs=vmem,
    )(exchanged)


def solution(mesh):
    big, squares = constants()

    def body(scan_pair):
        return on_device(scan_pair, jnp.asarray(big), jnp.asarray(squares))

    return jax.shard_map(
        body,
        mesh=mesh,
        in_specs=(P(None, None, "wide", "narrow"),),
        out_specs=P(None, None, "wide", "narrow"),
        check_vma=False,
    )
```

```python
import functools
import math

import jax
import jax.numpy as jnp
import ml_dtypes
import numpy as np
from jax import lax
from jax.experimental import pallas as pl
from jax.experimental.pallas import tpu as pltpu
from jax.sharding import PartitionSpec as P

magnitude_floor = 0.25
MESH = pl.DeviceIdType.MESH

LINE, PLANE, LANES, ROWS = 16, 32, 128, 512
LENGTH, POINTS = 2048, 16


def constants():
    ka = np.arange(128)
    j = np.arange(128)
    z1 = (j % 8) * 16 + j // 8
    big = np.exp(-2j * np.pi * ((ka[:, None] * z1[None, :]) % 128) / 128)
    forward_big = np.concatenate([big.real, big.imag], axis=0)
    back = np.conj(big).T
    inverse_big = np.concatenate([back.real, back.imag], axis=0)

    z0 = np.arange(POINTS)
    small = np.exp(-2j * np.pi * ((z0[:, None] * z0[None, :]) % POINTS) / POINTS) / math.sqrt(LENGTH)

    def lanes(matrix, columns):
        block = np.einsum("xw,zk->xzwk", columns, matrix).reshape(64, 64)
        return np.block([[block.real, block.imag], [-block.imag, block.real]])

    same, reverse = np.eye(4), np.eye(4)[::-1]
    turn = np.exp(-2j * np.pi * ka[:, None] * z0[None, :] / LENGTH)
    turn = np.tile(turn, (1, 4))
    turn_real = np.concatenate([turn.real, turn.real], axis=1)
    turn_imag = np.concatenate([-turn.imag, turn.imag], axis=1)
    factors = [lanes(small, same), lanes(small, reverse), lanes(np.conj(small), same)]
    turns = np.stack([turn_real, turn_imag, np.eye(128)[::-1]]).astype(np.float32)
    return (
        np.stack([left_factor(forward_big), left_factor(inverse_big)]),
        np.stack([right_factor(factor) for factor in factors]),
        turns,
    )


def pieces(matrix):
    high = matrix.astype(ml_dtypes.bfloat16)
    return high, (matrix - high.astype(np.float64)).astype(ml_dtypes.bfloat16)


def left_factor(matrix):
    high, low = pieces(matrix)
    return np.block([[high, high], [low, np.zeros_like(low)]])


def right_factor(matrix):
    high, low = pieces(matrix)
    return np.block([[high, low], [high, np.zeros_like(low)]])


def dot(left, right):
    return jnp.dot(
        left, right, precision=lax.Precision.HIGHEST, preferred_element_type=jnp.float32
    )


def split(value, axis):
    high = value.astype(jnp.bfloat16)
    low = (value - high.astype(jnp.float32)).astype(jnp.bfloat16)
    return jnp.concatenate([high, low], axis=axis)


def times_left(factor, value):
    product = jnp.dot(factor, split(value, 0), preferred_element_type=jnp.float32)
    return product[:256] + product[256:]


def times_right(value, factor):
    product = jnp.dot(split(value, 1), factor, preferred_element_type=jnp.float32)
    return product[:, :128] + product[:, 128:]


def correlate(blocks, first_device, big_ref, small_ref, turn_ref, roll):
    def swap(value):
        return roll(value, 64, 1)

    lane = lax.broadcasted_iota(jnp.int32, (128, LANES), 1)
    real_lane = lane < 64
    sign = jnp.where(real_lane, -1.0, 1.0).astype(jnp.float32)
    turn_real, turn_imag = turn_ref[0], turn_ref[1]

    both = times_left(big_ref[0], jnp.concatenate(blocks, axis=1))
    own, twin = [], []
    for n in range(4):
        upper = both[:128, n * 128 : (n + 1) * 128]
        lower = swap(both[128:, n * 128 : (n + 1) * 128])
        straight = upper + sign * lower
        conjugate = lower - sign * upper
        own.append(straight * turn_real + swap(straight) * turn_imag)
        twin.append(conjugate * turn_real + swap(conjugate) * turn_imag)
    mirrored = [
        jnp.where(first_device, twin[a], twin[b]) for a, b in ((0, 3), (3, 2), (2, 1), (1, 0))
    ]
    spectrum = times_right(jnp.concatenate(own, axis=0), small_ref[0])
    mirror_spectrum = times_right(jnp.concatenate(mirrored, axis=0), small_ref[1])
    normalized = []
    for n in range(4):
        s = spectrum[n * 128 : (n + 1) * 128]
        m = mirror_spectrum[n * 128 : (n + 1) * 128]
        first = (s + m) * 0.5
        half = (s - m) * 0.5
        turned = first * swap(half)
        plain = first * half
        cross = jnp.where(real_lane, turned - swap(turned), plain + swap(plain))
        square = cross * cross
        modulus = jnp.maximum(jnp.sqrt(square + swap(square)), magnitude_floor)
        normalized.append(cross / modulus)
    back = times_right(jnp.concatenate(normalized, axis=0), small_ref[2])
    turned_back = []
    for n in range(4):
        value = back[n * 128 : (n + 1) * 128]
        turned_back.append(value * turn_real - swap(value) * turn_imag)
    both = times_left(big_ref[1], jnp.concatenate(turned_back, axis=1))
    return [
        both[:128, n * 128 : (n + 1) * 128] + sign * swap(both[128:, n * 128 : (n + 1) * 128])
        for n in range(4)
    ]


def kernel(
    scan_hbm, big_hbm, small_hbm, turn_hbm, out_ref,
    scan_ref, big_ref, small_ref, turn_ref, rows, mid, landed, result, paired, arrived,
    send_line, recv_line, send_plane, recv_plane,
    send_core, recv_core, send_back, recv_back, local, load,
):
    narrow, wide = lax.axis_index("narrow"), lax.axis_index("wide")
    y_hi, core = narrow // 2, narrow % 2
    z, sheet = wide // 16, wide % 16
    line = core * 8 + z
    x, y = sheet // 4, y_hi * 4 + sheet % 4
    plane = x * 8 + y
    upper = narrow >= 2
    loads = [
        pltpu.make_async_copy(source, target, load.at[i])
        for i, (source, target) in enumerate(
            [
                (scan_hbm, scan_ref),
                (turn_hbm, turn_ref),
                (big_hbm, big_ref),
                (small_hbm, small_ref),
            ]
        )
    ]
    for copy in loads:
        copy.start()

    def line_peer(step):
        peer = (line + step) % LINE
        return peer, (y_hi * 2 + peer // 8, (peer % 8) * 16 + sheet)

    def plane_peer(step):
        to_x, to_y = (x + step // 8) % 4, (y + step) % 8
        return to_x * 8 + to_y, ((to_y // 4) * 2 + core, z * 16 + to_x * 4 + to_y % 4)

    def line_copy(far_x, step):
        peer, device = line_peer(step)
        first = pl.multiple_of(((x + far_x) % 4) * 8, 8)
        return pltpu.make_async_remote_copy(
            src_ref=rows.at[peer, pl.ds(first, 8)],
            dst_ref=mid.at[line, pl.ds(first, 8)],
            send_sem=send_line.at[far_x, step],
            recv_sem=recv_line.at[far_x, step],
            device_id=device,
            device_id_type=MESH,
        )

    def plane_copy(step):
        peer, device = plane_peer(step)
        return pltpu.make_async_remote_copy(
            src_ref=mid.at[:, peer],
            dst_ref=landed.at[x, y],
            send_sem=send_plane.at[step],
            recv_sem=recv_plane.at[step],
            device_id=device,
            device_id_type=MESH,
        )

    def each(low, high, act):
        def body(step, carry):
            act(step)
            return carry

        lax.fori_loop(low, high, body, 0)

    barrier = pltpu.get_barrier_semaphore()

    def greet(peer_of):
        def signal(step, carry):
            pl.semaphore_signal(
                barrier, inc=1, device_id=peer_of(step)[1], device_id_type=MESH
            )
            return carry

        return signal

    lax.fori_loop(1, PLANE, greet(plane_peer), 0)
    lax.fori_loop(1, LINE, greet(line_peer), 0)

    loads[0].wait()
    loads[1].wait()
    swap_matrix = turn_ref[2]
    given = scan_ref[...].reshape(LANES, ROWS)
    parts = [given[:, b * 128 : (b + 1) * 128] for b in range(4)]

    @pl.when(upper)
    def _():
        flipped = dot(jnp.concatenate(parts, axis=0), swap_matrix)
        backward = jnp.concatenate(
            [flipped[(3 - b) * 128 : (4 - b) * 128].T for b in range(4)], axis=0
        )
        rows[...] = pltpu.roll(backward, 1, 0).reshape(LINE, PLANE, LANES)

    @pl.when(jnp.logical_not(upper))
    def _():
        forward = jnp.concatenate([part.T for part in parts], axis=0)
        rows[...] = forward.reshape(LINE, PLANE, LANES)

    pl.semaphore_wait(barrier, LINE + PLANE - 2)

    parts_order = (2, 1, 3, 0)
    for far_x in parts_order:
        each(1, LINE, lambda step: line_copy(far_x, step).start())
    own = pltpu.make_async_copy(rows.at[line], mid.at[line], local.at[0])
    own.start()
    own.wait()
    for far_x in parts_order:
        each(1, LINE, lambda step: line_copy(far_x, step).wait_recv())
        each(max(far_x * 8, 1), far_x * 8 + 8, lambda step: plane_copy(step).start())
    own = pltpu.make_async_copy(mid.at[:, plane], landed.at[x, y], local.at[1])
    own.start()
    own.wait()
    for far_x in parts_order:
        each(1, LINE, lambda step: line_copy(far_x, step).wait_send())
    each(1, PLANE, lambda step: plane_copy(step).wait())

    blocks = [
        landed[
            :, 4 * (n // 2) : 4 * (n // 2) + 4, 8 * (n % 2) : 8 * (n % 2) + 8, :
        ].reshape(128, LANES)
        for n in range(4)
    ]
    loads[2].wait()
    loads[3].wait()
    first_device = line + plane == 0
    outcome = correlate(blocks, first_device, big_ref, small_ref, turn_ref, pltpu.roll)
    for n in range(4):
        result[n % 2, (n // 2) * 128 : (n // 2) * 128 + 128, :] = outcome[n]

    place = z * 32 + plane
    place_mirror = (256 - place) % 256
    other = 1 - core
    slots = (core, jnp.where(place == 0, core, other))
    partner = (y_hi * 2 + other, wide)

    def half(half_index):
        return pl.ds(half_index * 128, 128)

    swaps = [
        pltpu.make_async_remote_copy(
            src_ref=result.at[other, half(h)],
            dst_ref=paired.at[slots[h], half(h)],
            send_sem=send_core.at[h],
            recv_sem=recv_core.at[h],
            device_id=partner,
            device_id_type=MESH,
        )
        for h in range(2)
    ]
    keeps = [
        pltpu.make_async_copy(
            result.at[core, half(h)], paired.at[slots[h], half(h)], local.at[2 + h]
        )
        for h in range(2)
    ]
    for copy in swaps + keeps:
        copy.start()
    for copy in swaps + keeps:
        copy.wait()

    for far_x in (2, 1, 3, 0):
        to_x = (x + far_x) % 4

        def row_of_chips(step, carry, to_x=to_x, far_x=far_x):
            bend = (step + 1) // 2
            to_y = (y + 4 + jnp.where(step % 2 == 1, -bend, bend)) % 8
            to_half, to_sheet = to_y // 4, to_x * 4 + to_y % 4
            to_place = jnp.where(to_half == 0, place, place_mirror)
            for far_z in (4, 3, 5, 2, 6, 1, 7, 0):
                to_z = (z + far_z) % 8
                copy = pltpu.make_async_remote_copy(
                    src_ref=paired.at[:, (to_half * 16 + to_sheet) * 8 + to_z],
                    dst_ref=arrived.at[:, to_place],
                    send_sem=send_back.at[0],
                    recv_sem=recv_back.at[0],
                    device_id=(to_half * 2 + core, to_z * 16 + to_sheet),
                    device_id_type=MESH,
                )
                if far_x == 0 and far_z == 0:
                    pl.when(step < 7)(copy.start)
                else:
                    copy.start()
            return carry

        lax.fori_loop(0, 8, row_of_chips, 0)
    own = pltpu.make_async_copy(
        paired.at[:, plane_row(y_hi, sheet, z)],
        arrived.at[:, jnp.where(y_hi == 0, place, place_mirror)],
        local.at[4],
    )
    own.start()
    own.wait()
    everything = arrived.at[:, pl.ds(0, 255)]
    pltpu.make_async_copy(everything, everything, send_back.at[0]).wait()
    pltpu.make_async_copy(everything, everything, recv_back.at[0]).wait()
    out_ref[...] = arrived[...].reshape(ROWS, LANES)


def plane_row(y_hi, sheet, z):
    return (y_hi * 16 + sheet) * 8 + z


def turn_kernel(rows_ref, out_ref):
    rows = rows_ref[...]
    final = jnp.concatenate([rows[b * 128 : (b + 1) * 128].T for b in range(4)], axis=1)
    out_ref[...] = final.reshape(out_ref.shape)


def on_device(scan_pair, big, small, turns):
    vmem = pl.BlockSpec(memory_space=pltpu.VMEM)
    dma = pltpu.SemaphoreType.DMA
    exchanged = pl.pallas_call(
        kernel,
        out_shape=jax.ShapeDtypeStruct((ROWS, LANES), jnp.float32),
        in_specs=[pl.BlockSpec(memory_space=pl.ANY)] * 4,
        out_specs=vmem,
        scratch_shapes=[
            pltpu.VMEM(scan_pair.shape, jnp.float32),
            pltpu.VMEM(big.shape, jnp.bfloat16),
            pltpu.VMEM(small.shape, jnp.bfloat16),
            pltpu.VMEM(turns.shape, jnp.float32),
            pltpu.VMEM((LINE, PLANE, LANES), jnp.float32),
            pltpu.VMEM((LINE, PLANE, LANES), jnp.float32),
            pltpu.VMEM((4, 8, LINE, LANES), jnp.float32),
            pltpu.VMEM((2, 256, LANES), jnp.float32),
            pltpu.VMEM((2, 256, LANES), jnp.float32),
            pltpu.VMEM((2, 256, LANES), jnp.float32),
            dma((4, LINE)), dma((4, LINE)), dma((PLANE,)), dma((PLANE,)),
            dma((2,)), dma((2,)), dma((1,)), dma((1,)), dma((5,)), dma((4,)),
        ],
        compiler_params=pltpu.CompilerParams(collective_id=0, has_side_effects=True),
    )(scan_pair, big, small, turns)
    return pl.pallas_call(
        turn_kernel,
        out_shape=jax.ShapeDtypeStruct(scan_pair.shape, jnp.float32),
        in_specs=[vmem],
        out_specs=vmem,
    )(exchanged)


def solution(mesh):
    tables = constants()

    def body(scan_pair):
        return on_device(scan_pair, *(jnp.asarray(table) for table in tables))

    return jax.shard_map(
        body,
        mesh=mesh,
        in_specs=(P(None, None, "wide", "narrow"),),
        out_specs=P(None, None, "wide", "narrow"),
        check_vma=False,
    )
```

```python
import functools
import math

import jax
import jax.numpy as jnp
import ml_dtypes
import numpy as np
from jax import lax
from jax.experimental import pallas as pl
from jax.experimental.pallas import tpu as pltpu
from jax.sharding import PartitionSpec as P

magnitude_floor = 0.25
MESH = pl.DeviceIdType.MESH

LINE, PLANE, LANES, ROWS = 16, 32, 128, 512
LENGTH, POINTS = 2048, 16


def constants():
    ka = np.arange(128)
    j = np.arange(128)
    z1 = (j % 8) * 16 + j // 8
    big = np.exp(-2j * np.pi * ((ka[:, None] * z1[None, :]) % 128) / 128)
    forward_big = np.concatenate([big.real, big.imag], axis=0)
    back = np.conj(big).T
    inverse_big = np.concatenate([back.real, back.imag], axis=0)

    z0 = np.arange(POINTS)
    small = np.exp(-2j * np.pi * ((z0[:, None] * z0[None, :]) % POINTS) / POINTS) / math.sqrt(LENGTH)

    def lanes(matrix, columns):
        block = np.einsum("xw,zk->xzwk", columns, matrix).reshape(64, 64)
        return np.block([[block.real, block.imag], [-block.imag, block.real]])

    same, reverse = np.eye(4), np.eye(4)[::-1]
    turn = np.exp(-2j * np.pi * ka[:, None] * z0[None, :] / LENGTH)
    turn = np.tile(turn, (1, 4))
    turn_real = np.concatenate([turn.real, turn.real], axis=1)
    turn_imag = np.concatenate([-turn.imag, turn.imag], axis=1)
    factors = [lanes(small, same), lanes(small, reverse), lanes(np.conj(small), same)]
    turns = np.stack([turn_real, turn_imag, np.eye(128)[::-1]]).astype(np.float32)
    return (
        np.stack([left_factor(forward_big), left_factor(inverse_big)]),
        np.stack([right_factor(factor) for factor in factors]),
        turns,
    )


def pieces(matrix):
    high = matrix.astype(ml_dtypes.bfloat16)
    return high, (matrix - high.astype(np.float64)).astype(ml_dtypes.bfloat16)


def left_factor(matrix):
    high, low = pieces(matrix)
    return np.block([[high, high], [low, np.zeros_like(low)]])


def right_factor(matrix):
    high, low = pieces(matrix)
    return np.block([[high, low], [high, np.zeros_like(low)]])


def dot(left, right):
    return jnp.dot(
        left, right, precision=lax.Precision.HIGHEST, preferred_element_type=jnp.float32
    )


def split(value, axis):
    high = value.astype(jnp.bfloat16)
    low = (value - high.astype(jnp.float32)).astype(jnp.bfloat16)
    return jnp.concatenate([high, low], axis=axis)


def times_left(factor, value):
    product = jnp.dot(factor, split(value, 0), preferred_element_type=jnp.float32)
    return product[:256] + product[256:]


def times_right(value, factor):
    product = jnp.dot(split(value, 1), factor, preferred_element_type=jnp.float32)
    return product[:, :128] + product[:, 128:]


def correlate(blocks, first_device, big_ref, small_ref, turn_ref, roll):
    def swap(value):
        return roll(value, 64, 1)

    lane = lax.broadcasted_iota(jnp.int32, (128, LANES), 1)
    real_lane = lane < 64
    sign = jnp.where(real_lane, -1.0, 1.0).astype(jnp.float32)
    turn_real, turn_imag = turn_ref[0], turn_ref[1]

    both = times_left(big_ref[0], jnp.concatenate(blocks, axis=1))
    own, twin = [], []
    for n in range(4):
        upper = both[:128, n * 128 : (n + 1) * 128]
        lower = swap(both[128:, n * 128 : (n + 1) * 128])
        straight = upper + sign * lower
        conjugate = lower - sign * upper
        own.append(straight * turn_real + swap(straight) * turn_imag)
        twin.append(conjugate * turn_real + swap(conjugate) * turn_imag)
    mirrored = [
        jnp.where(first_device, twin[a], twin[b]) for a, b in ((0, 3), (3, 2), (2, 1), (1, 0))
    ]
    spectrum = times_right(jnp.concatenate(own, axis=0), small_ref[0])
    mirror_spectrum = times_right(jnp.concatenate(mirrored, axis=0), small_ref[1])
    normalized = []
    for n in range(4):
        s = spectrum[n * 128 : (n + 1) * 128]
        m = mirror_spectrum[n * 128 : (n + 1) * 128]
        first = (s + m) * 0.5
        half = (s - m) * 0.5
        turned = first * swap(half)
        plain = first * half
        cross = jnp.where(real_lane, turned - swap(turned), plain + swap(plain))
        square = cross * cross
        modulus = jnp.maximum(jnp.sqrt(square + swap(square)), magnitude_floor)
        normalized.append(cross / modulus)
    back = times_right(jnp.concatenate(normalized, axis=0), small_ref[2])
    turned_back = []
    for n in range(4):
        value = back[n * 128 : (n + 1) * 128]
        turned_back.append(value * turn_real - swap(value) * turn_imag)
    return turned_back


def finish(blocks, big_ref, roll):
    lane = lax.broadcasted_iota(jnp.int32, (128, LANES), 1)
    sign = jnp.where(lane < 64, -1.0, 1.0).astype(jnp.float32)
    both = times_left(big_ref[1], jnp.concatenate(blocks, axis=1))
    return [
        both[:128, n * 128 : (n + 1) * 128] + sign * roll(both[128:, n * 128 : (n + 1) * 128], 64, 1)
        for n in range(len(blocks))
    ]


def kernel(
    scan_hbm, big_hbm, small_hbm, turn_hbm, out_ref,
    scan_ref, big_ref, small_ref, turn_ref, rows, mid, landed, result, paired, arrived,
    send_line, recv_line, send_plane, recv_plane,
    send_core, recv_core, send_back, recv_back, local, load,
):
    narrow, wide = lax.axis_index("narrow"), lax.axis_index("wide")
    y_hi, core = narrow // 2, narrow % 2
    z, sheet = wide // 16, wide % 16
    line = core * 8 + z
    x, y = sheet // 4, y_hi * 4 + sheet % 4
    plane = x * 8 + y
    upper = narrow >= 2
    loads = [
        pltpu.make_async_copy(source, target, load.at[i])
        for i, (source, target) in enumerate(
            [
                (scan_hbm, scan_ref),
                (turn_hbm, turn_ref),
                (big_hbm, big_ref),
                (small_hbm, small_ref),
            ]
        )
    ]
    for copy in loads:
        copy.start()

    def line_peer(step):
        peer = (line + step) % LINE
        return peer, (y_hi * 2 + peer // 8, (peer % 8) * 16 + sheet)

    def plane_peer(step):
        to_x, to_y = (x + step // 8) % 4, (y + step) % 8
        return to_x * 8 + to_y, ((to_y // 4) * 2 + core, z * 16 + to_x * 4 + to_y % 4)

    def line_copy(far_x, step):
        peer, device = line_peer(step)
        first = pl.multiple_of(((x + far_x) % 4) * 8, 8)
        return pltpu.make_async_remote_copy(
            src_ref=rows.at[peer, pl.ds(first, 8)],
            dst_ref=mid.at[line, pl.ds(first, 8)],
            send_sem=send_line.at[far_x, step],
            recv_sem=recv_line.at[far_x, step],
            device_id=device,
            device_id_type=MESH,
        )

    def plane_copy(step):
        peer, device = plane_peer(step)
        return pltpu.make_async_remote_copy(
            src_ref=mid.at[:, peer],
            dst_ref=landed.at[x, y],
            send_sem=send_plane.at[step],
            recv_sem=recv_plane.at[step],
            device_id=device,
            device_id_type=MESH,
        )

    def each(low, high, act):
        def body(step, carry):
            act(step)
            return carry

        lax.fori_loop(low, high, body, 0)

    barrier = pltpu.get_barrier_semaphore()

    def greet(peer_of):
        def signal(step, carry):
            pl.semaphore_signal(
                barrier, inc=1, device_id=peer_of(step)[1], device_id_type=MESH
            )
            return carry

        return signal

    lax.fori_loop(1, PLANE, greet(plane_peer), 0)
    lax.fori_loop(1, LINE, greet(line_peer), 0)

    loads[0].wait()
    loads[1].wait()
    swap_matrix = turn_ref[2]
    given = scan_ref[...].reshape(LANES, ROWS)
    parts = [given[:, b * 128 : (b + 1) * 128] for b in range(4)]

    @pl.when(upper)
    def _():
        flipped = dot(jnp.concatenate(parts, axis=0), swap_matrix)
        backward = jnp.concatenate(
            [flipped[(3 - b) * 128 : (4 - b) * 128].T for b in range(4)], axis=0
        )
        rows[...] = pltpu.roll(backward, 1, 0).reshape(LINE, PLANE, LANES)

    @pl.when(jnp.logical_not(upper))
    def _():
        forward = jnp.concatenate([part.T for part in parts], axis=0)
        rows[...] = forward.reshape(LINE, PLANE, LANES)

    pl.semaphore_wait(barrier, LINE + PLANE - 2)

    parts_order = (2, 1, 3, 0)
    for far_x in parts_order:
        each(1, LINE, lambda step: line_copy(far_x, step).start())
    own = pltpu.make_async_copy(rows.at[line], mid.at[line], local.at[0])
    own.start()
    own.wait()
    for far_x in parts_order:
        each(1, LINE, lambda step: line_copy(far_x, step).wait_recv())
        each(max(far_x * 8, 1), far_x * 8 + 8, lambda step: plane_copy(step).start())
    own = pltpu.make_async_copy(mid.at[:, plane], landed.at[x, y], local.at[1])
    own.start()
    own.wait()
    for far_x in parts_order:
        each(1, LINE, lambda step: line_copy(far_x, step).wait_send())
    each(1, PLANE, lambda step: plane_copy(step).wait())

    blocks = [
        landed[
            :, 4 * (n // 2) : 4 * (n // 2) + 4, 8 * (n % 2) : 8 * (n % 2) + 8, :
        ].reshape(128, LANES)
        for n in range(4)
    ]
    loads[2].wait()
    loads[3].wait()
    first_device = line + plane == 0
    turned = correlate(blocks, first_device, big_ref, small_ref, turn_ref, pltpu.roll)
    at_zero = core == 0
    given_away = [jnp.where(at_zero, turned[2 * h + 1], turned[2 * h]) for h in range(2)]
    kept = [jnp.where(at_zero, turned[2 * h], turned[2 * h + 1]) for h in range(2)]

    place = z * 32 + plane
    place_mirror = (256 - place) % 256
    other = 1 - core
    slots = (core, jnp.where(place == 0, core, other))
    partner = (y_hi * 2 + other, wide)

    def half(half_index):
        return pl.ds(half_index * 128, 128)

    swaps = [
        pltpu.make_async_remote_copy(
            src_ref=result.at[half(h)],
            dst_ref=paired.at[slots[h], half(h)],
            send_sem=send_core.at[h],
            recv_sem=recv_core.at[h],
            device_id=partner,
            device_id_type=MESH,
        )
        for h in range(2)
    ]
    for h, value in enumerate(finish(given_away, big_ref, pltpu.roll)):
        result[half(h)] = value
    for copy in swaps:
        copy.start()
    for h, value in enumerate(finish(kept, big_ref, pltpu.roll)):
        paired[slots[h], half(h)] = value
    for copy in swaps:
        copy.wait()

    for far_x in (2, 1, 3, 0):
        to_x = (x + far_x) % 4

        def row_of_chips(step, carry, to_x=to_x, far_x=far_x):
            bend = (step + 1) // 2
            to_y = (y + 4 + jnp.where(step % 2 == 1, -bend, bend)) % 8
            to_half, to_sheet = to_y // 4, to_x * 4 + to_y % 4
            to_place = jnp.where(to_half == 0, place, place_mirror)
            for far_z in (4, 3, 5, 2, 6, 1, 7, 0):
                to_z = (z + far_z) % 8
                copy = pltpu.make_async_remote_copy(
                    src_ref=paired.at[:, (to_half * 16 + to_sheet) * 8 + to_z],
                    dst_ref=arrived.at[:, to_place],
                    send_sem=send_back.at[0],
                    recv_sem=recv_back.at[0],
                    device_id=(to_half * 2 + core, to_z * 16 + to_sheet),
                    device_id_type=MESH,
                )
                if far_x == 0 and far_z == 0:
                    pl.when(step < 7)(copy.start)
                else:
                    copy.start()
            return carry

        lax.fori_loop(0, 8, row_of_chips, 0)
    own = pltpu.make_async_copy(
        paired.at[:, plane_row(y_hi, sheet, z)],
        arrived.at[:, jnp.where(y_hi == 0, place, place_mirror)],
        local.at[2],
    )
    own.start()
    own.wait()
    everything = arrived.at[:, pl.ds(0, 255)]
    pltpu.make_async_copy(everything, everything, send_back.at[0]).wait()
    pltpu.make_async_copy(everything, everything, recv_back.at[0]).wait()
    out_ref[...] = arrived[...].reshape(ROWS, LANES)


def plane_row(y_hi, sheet, z):
    return (y_hi * 16 + sheet) * 8 + z


def turn_kernel(rows_ref, out_ref):
    rows = rows_ref[...]
    final = jnp.concatenate([rows[b * 128 : (b + 1) * 128].T for b in range(4)], axis=1)
    out_ref[...] = final.reshape(out_ref.shape)


def on_device(scan_pair, big, small, turns):
    vmem = pl.BlockSpec(memory_space=pltpu.VMEM)
    dma = pltpu.SemaphoreType.DMA
    exchanged = pl.pallas_call(
        kernel,
        out_shape=jax.ShapeDtypeStruct((ROWS, LANES), jnp.float32),
        in_specs=[pl.BlockSpec(memory_space=pl.ANY)] * 4,
        out_specs=vmem,
        scratch_shapes=[
            pltpu.VMEM(scan_pair.shape, jnp.float32),
            pltpu.VMEM(big.shape, jnp.bfloat16),
            pltpu.VMEM(small.shape, jnp.bfloat16),
            pltpu.VMEM(turns.shape, jnp.float32),
            pltpu.VMEM((LINE, PLANE, LANES), jnp.float32),
            pltpu.VMEM((LINE, PLANE, LANES), jnp.float32),
            pltpu.VMEM((4, 8, LINE, LANES), jnp.float32),
            pltpu.VMEM((256, LANES), jnp.float32),
            pltpu.VMEM((2, 256, LANES), jnp.float32),
            pltpu.VMEM((2, 256, LANES), jnp.float32),
            dma((4, LINE)), dma((4, LINE)), dma((PLANE,)), dma((PLANE,)),
            dma((2,)), dma((2,)), dma((1,)), dma((1,)), dma((3,)), dma((4,)),
        ],
        compiler_params=pltpu.CompilerParams(collective_id=0, has_side_effects=True),
    )(scan_pair, big, small, turns)
    return pl.pallas_call(
        turn_kernel,
        out_shape=jax.ShapeDtypeStruct(scan_pair.shape, jnp.float32),
        in_specs=[vmem],
        out_specs=vmem,
    )(exchanged)


def solution(mesh):
    tables = constants()

    def body(scan_pair):
        return on_device(scan_pair, *(jnp.asarray(table) for table in tables))

    return jax.shard_map(
        body,
        mesh=mesh,
        in_specs=(P(None, None, "wide", "narrow"),),
        out_specs=P(None, None, "wide", "narrow"),
        check_vma=False,
    )
```
